256 devices in a mesh: replica: 16 (over z_hi, x), dp: 2 (over core), shard: 8 (over y, z_lo).
Axes of the slice: x: 4, y: 4, z: 8 (z_hi: 4, z_lo: 2; z = z_hi * 2 + z_lo), core: 2. Of those that a mesh axis runs over, the one named last changes fastest.
Arguments:
- round_index: int32 [2], replicated, may hold values from 0 to 2999
- activations: bfloat16 [2, 16, 2048, 4096], P(None, 'replica', ('dp', 'shard')), may hold values from -6 to 6
- cotangents: bfloat16 [2, 16, 2048, 2048], P(None, 'replica', 'dp', 'shard'), may hold values from -0.119628906 to 0.119628906
- params: float32 [16, 4096, 2048], P('replica', 'dp', 'shard'), may hold values from -6 to 6
- momentum: float32 [16, 4096, 2048], P('replica', 'dp', 'shard'), may hold values from -3 to 3
Outputs:
- new_params: float32 [16, 4096, 2048], P('replica', 'dp', 'shard')
- new_momentum: float32 [16, 4096, 2048], P('replica', 'dp', 'shard')
The draws below stay inside these ranges and needn't reach their ends.
All inputs are finite; a program needn't handle non-finite values.
Results may differ from the reference program's by a relative error of at most 0.0003.
Values may be sent and summed in bfloat16 or wider, within the bound.
A program may use at most 128 MiB of HBM per device.

```python
import jax
import jax.numpy as jnp
from jax import lax

D = 4096
KV = 2048
ROUNDS = 2
TOKENS = 2048
N_REPLICA = 16


def block_scale(stream_key, extent, shards, low, high):
    level = 1.0
    for position, parts in shards:
        heights = jax.random.uniform(jax.random.fold_in(jax.random.fold_in(stream_key, 6), position), (parts,), jnp.float32, low / len(shards), high / len(shards))
        level = level * jnp.repeat(jnp.exp(heights), extent[position] // parts).reshape((-1,) + (1,) * (len(extent) - 1 - position))
    return level


def normal_values(key, shape, deviation, most, pieces=(), kind=jnp.bfloat16):
    factor_of = block_scale(key, shape, pieces, -0.22, 0.18) if pieces else 1.0
    drawn = jax.random.normal(key, shape, jnp.float32) * deviation * factor_of
    return jnp.minimum(jnp.maximum(drawn, -most), most).astype(kind)


def setup_inputs(seed: int = 0) -> dict:
    keys = jax.random.split(jax.random.key(seed), 6)
    return {
        "round_index": jax.random.randint(keys[0], (ROUNDS,), 0, 3000).astype(jnp.int32),
        "activations": normal_values(keys[1], (ROUNDS, N_REPLICA, TOKENS, D), 1.0, 6.0, ((1, 16), (2, 16))),
        "cotangents": normal_values(keys[2], (ROUNDS, N_REPLICA, TOKENS, KV), 0.02, 0.119628906, ((1, 16), (2, 2), (3, 8))),
        "params": normal_values(keys[3], (N_REPLICA, D, KV), 1.0, 6.0, ((0, 16), (1, 2), (2, 8)), jnp.float32),
        "momentum": normal_values(keys[4], (N_REPLICA, D, KV), 0.5, 3.0, ((0, 16), (1, 2), (2, 8)), jnp.float32),
    }


momentum_coef = 0.9
step_size = 0.25

def replica_grad(pair):
    inputs_block, cot_block = pair
    return jnp.dot(inputs_block.T, cot_block, preferred_element_type=jnp.float32)

def reference(round_index, activations, cotangents, params, momentum):
    replica_ids = jnp.arange(params.shape[0], dtype=jnp.int32)
    for k in range(ROUNDS):
        grad = lax.map(replica_grad, (activations[k], cotangents[k]))
        momentum = momentum_coef * momentum + grad
        stepped = params - step_size * (grad + momentum_coef * momentum)
        offset = jnp.left_shift(jnp.int32(1), (round_index[k] % 3).astype(jnp.int32))
        partner_ids = jnp.bitwise_xor(replica_ids, offset).astype(jnp.int32)
        partner = jnp.take(stepped, partner_ids, axis=0)
        params = (stepped + partner) * 0.5
    return (params, momentum)
```

```python
from functools import partial

import jax
import jax.numpy as jnp
from jax import lax
from jax.sharding import PartitionSpec as P

ROUNDS = 2


momentum_coef = 0.9
step_size = 0.25


def swapped(block, axis, stride):
    count = lax.axis_size(axis)
    route = []
    for low in range(count):
        high = low | 1 << stride
        if high != low and high < count:
            route += [(low, high), (high, low)]
    return lax.ppermute(block, axis, route)


def shifted(block, axis, route_of):
    count = lax.axis_size(axis)
    return lax.ppermute(block, axis, [(i, route_of(i)) for i in range(count)])


def gather_tokens(rows):
    count = lax.axis_size("shard")
    ny = count // 2
    half = rows.shape[0] // 2

    def move(y_step, z_flip):
        def route_of(s):
            y, z = divmod(s, 2)
            return ((y + y_step) % ny) * 2 + (z ^ z_flip)
        return route_of

    z_in = shifted(rows, "shard", move(0, 1))
    from_dn = shifted(rows, "shard", move(1, 0))
    from_up = shifted(rows, "shard", move(-1, 0))
    z_from_dn = shifted(z_in, "shard", move(1, 0))
    z_from_up = shifted(z_in, "shard", move(-1, 0))
    far_a = shifted(from_dn[:half], "shard", move(1, 0))
    far_b = shifted(from_up[half:], "shard", move(-1, 0))
    z_far_a = shifted(z_from_dn[:half], "shard", move(1, 0))
    z_far_b = shifted(z_from_up[half:], "shard", move(-1, 0))
    blocks = [rows, z_in, from_dn, z_from_dn, from_up, z_from_up,
              jnp.concatenate([far_a, far_b]), jnp.concatenate([z_far_a, z_far_b])]
    s = lax.axis_index("shard")
    y, z = s // 2, s % 2
    sources = [
        s,
        y * 2 + (1 - z),
        ((y - 1) % ny) * 2 + z,
        ((y - 1) % ny) * 2 + (1 - z),
        ((y + 1) % ny) * 2 + z,
        ((y + 1) % ny) * 2 + (1 - z),
        ((y + 2) % ny) * 2 + z,
        ((y + 2) % ny) * 2 + (1 - z),
    ]
    return jnp.concatenate(blocks), sources


def gradient(activations, cotangents, k):
    tok_rows = activations[k, 0]
    cot_block = cotangents[k, 0]
    block = tok_rows.shape[0]
    gathered, sources = gather_tokens(tok_rows)
    cot_rel = jnp.concatenate(
        [lax.dynamic_slice_in_dim(cot_block, src * block, block, axis=0) for src in sources]
    )
    d = lax.axis_index("dp")
    n_rows = tok_rows.shape[1] // 2
    other = lax.dynamic_slice_in_dim(gathered, (1 - d) * n_rows, n_rows, axis=1)
    mine = lax.dynamic_slice_in_dim(gathered, d * n_rows, n_rows, axis=1)
    dims = (((0,), (0,)), ((), ()))
    part_other = lax.dot_general(other, cot_rel, dims, preferred_element_type=jnp.float32)
    sent = lax.ppermute(part_other, "dp", [(0, 1), (1, 0)])
    part_mine = lax.dot_general(mine, cot_rel, dims, preferred_element_type=jnp.float32)
    return part_mine + sent


def trade_far(values):
    count = lax.axis_size("replica")
    nx = 4
    half = values.shape[0] // 2

    def hop(step):
        def route_of(r):
            zh, x = divmod(r, nx)
            return zh * nx + (x + step) % nx
        return route_of

    a = shifted(shifted(values[:half], "replica", hop(1)), "replica", hop(1))
    b = shifted(shifted(values[half:], "replica", hop(-1)), "replica", hop(-1))
    return jnp.concatenate([a, b])


def trade_with(level, values):
    if level == 1:
        return trade_far(values)
    return swapped(values, "replica", level)


def advance(round_index, k, grad, params_now, moment_now):
    moment_next = momentum_coef * moment_now + grad
    stepped = params_now - step_size * (grad + momentum_coef * moment_next)
    branches = [partial(trade_with, level) for level in range(3)]
    partner = lax.switch(round_index[k] % 3, branches, stepped)
    return ((stepped + partner) * 0.5, moment_next)


def local(round_index, activations, cotangents, params, momentum):
    params_now = params[0]
    moment_now = momentum[0]
    grads = [gradient(activations, cotangents, k) for k in range(ROUNDS)]
    for k in range(ROUNDS):
        params_now, moment_now = advance(round_index, k, grads[k], params_now, moment_now)
    return (params_now[None], moment_now[None])


def solution(mesh):
    in_specs = (
        P(),
        P(None, "replica", ("dp", "shard"), None),
        P(None, "replica", "dp", "shard"),
        P("replica", "dp", "shard"),
        P("replica", "dp", "shard"),
    )
    out_specs = (P("replica", "dp", "shard"), P("replica", "dp", "shard"))
    return jax.shard_map(local, mesh=mesh, in_specs=in_specs, out_specs=out_specs, check_vma=False)
```

```python
from functools import partial

import jax
import jax.numpy as jnp
from jax import lax
from jax.sharding import PartitionSpec as P

ROUNDS = 2


momentum_coef = 0.9
step_size = 0.25


def swapped(block, axis, stride):
    count = lax.axis_size(axis)
    route = []
    for low in range(count):
        high = low | 1 << stride
        if high != low and high < count:
            route += [(low, high), (high, low)]
    return lax.ppermute(block, axis, route)


def shifted(block, axis, route_of):
    count = lax.axis_size(axis)
    return lax.ppermute(block, axis, [(i, route_of(i)) for i in range(count)])


def gather_tokens(rows):
    count = lax.axis_size("shard")
    ny = count // 2
    half = rows.shape[0] // 2

    def move(y_step, z_flip):
        def route_of(s):
            y, z = divmod(s, 2)
            return ((y + y_step) % ny) * 2 + (z ^ z_flip)
        return route_of

    z_in = shifted(rows, "shard", move(0, 1))
    from_dn = shifted(rows, "shard", move(1, 0))
    from_up = shifted(rows, "shard", move(-1, 0))
    z_from_dn = shifted(z_in, "shard", move(1, 0))
    z_from_up = shifted(z_in, "shard", move(-1, 0))
    far_a = shifted(from_dn[:half], "shard", move(1, 0))
    far_b = shifted(from_up[half:], "shard", move(-1, 0))
    z_far_a = shifted(z_from_dn[:half], "shard", move(1, 0))
    z_far_b = shifted(z_from_up[half:], "shard", move(-1, 0))
    blocks = [rows, z_in, from_dn, z_from_dn, from_up, z_from_up,
              jnp.concatenate([far_a, far_b]), jnp.concatenate([z_far_a, z_far_b])]
    s = lax.axis_index("shard")
    y, z = s // 2, s % 2
    sources = [
        s,
        y * 2 + (1 - z),
        ((y - 1) % ny) * 2 + z,
        ((y - 1) % ny) * 2 + (1 - z),
        ((y + 1) % ny) * 2 + z,
        ((y + 1) % ny) * 2 + (1 - z),
        ((y + 2) % ny) * 2 + z,
        ((y + 2) % ny) * 2 + (1 - z),
    ]
    return jnp.concatenate(blocks), sources


def gradient(activations, cotangents, k):
    tok_rows = activations[k, 0]
    cot_block = cotangents[k, 0]
    block = tok_rows.shape[0]
    gathered, sources = gather_tokens(tok_rows)
    cot_rel = jnp.concatenate(
        [lax.dynamic_slice_in_dim(cot_block, src * block, block, axis=0) for src in sources]
    )
    d = lax.axis_index("dp")
    n_rows = tok_rows.shape[1] // 2
    other = lax.dynamic_slice_in_dim(gathered, (1 - d) * n_rows, n_rows, axis=1)
    mine = lax.dynamic_slice_in_dim(gathered, d * n_rows, n_rows, axis=1)
    dims = (((0,), (0,)), ((), ()))
    part_other = lax.dot_general(other, cot_rel, dims, preferred_element_type=jnp.float32)
    sent = lax.ppermute(part_other, "dp", [(0, 1), (1, 0)])
    part_mine = lax.dot_general(mine, cot_rel, dims, preferred_element_type=jnp.float32)
    return part_mine + sent


def trade_far(values):
    count = lax.axis_size("replica")
    nx = 4
    half = values.shape[0] // 2

    def hop(step):
        def route_of(r):
            zh, x = divmod(r, nx)
            return zh * nx + (x + step) % nx
        return route_of

    a = shifted(shifted(values[:half], "replica", hop(1)), "replica", hop(1))
    b = shifted(shifted(values[half:], "replica", hop(-1)), "replica", hop(-1))
    return jnp.concatenate([a, b])


def trade_with(level, values):
    if level == 1:
        return trade_far(values)
    return swapped(values, "replica", level)


def stepped_of(grad, params_now, moment_now):
    moment_next = momentum_coef * moment_now + grad
    stepped = params_now - step_size * (grad + momentum_coef * moment_next)
    return stepped, moment_next


def trade_and_grad(level, stepped, activations, cotangents, k):
    return trade_with(level, stepped), gradient(activations, cotangents, k)


def local(round_index, activations, cotangents, params, momentum):
    params_now = params[0]
    moment_now = momentum[0]
    grad = gradient(activations, cotangents, 0)
    for k in range(ROUNDS):
        stepped, moment_now = stepped_of(grad, params_now, moment_now)
        level = round_index[k] % 3
        if k + 1 < ROUNDS:
            branches = [partial(trade_and_grad, lv) for lv in range(3)]
            partner, grad = lax.switch(level, branches, stepped, activations, cotangents, k + 1)
        else:
            branches = [partial(trade_with, lv) for lv in range(3)]
            partner = lax.switch(level, branches, stepped)
        params_now = (stepped + partner) * 0.5
    return (params_now[None], moment_now[None])


def solution(mesh):
    in_specs = (
        P(),
        P(None, "replica", ("dp", "shard"), None),
        P(None, "replica", "dp", "shard"),
        P("replica", "dp", "shard"),
        P("replica", "dp", "shard"),
    )
    out_specs = (P("replica", "dp", "shard"), P("replica", "dp", "shard"))
    return jax.shard_map(local, mesh=mesh, in_specs=in_specs, out_specs=out_specs, check_vma=False)
```

```python
from functools import partial

import jax
import jax.numpy as jnp
from jax import lax
from jax.sharding import PartitionSpec as P

ROUNDS = 2
CHUNKS = 2


momentum_coef = 0.9
step_size = 0.25


def swapped(block, axis, stride):
    count = lax.axis_size(axis)
    route = []
    for low in range(count):
        high = low | 1 << stride
        if high != low and high < count:
            route += [(low, high), (high, low)]
    return lax.ppermute(block, axis, route)


def shifted(block, axis, route_of):
    count = lax.axis_size(axis)
    return lax.ppermute(block, axis, [(i, route_of(i)) for i in range(count)])


def gather_tokens(rows, side=None):
    count = lax.axis_size("shard")
    ny = count // 2
    half = rows.shape[0] // 2

    def move(y_step, z_flip):
        def route_of(s):
            y, z = divmod(s, 2)
            return ((y + y_step) % ny) * 2 + (z ^ z_flip)
        return route_of

    z_in = shifted(rows, "shard", move(0, 1))
    from_dn = shifted(rows, "shard", move(1, 0))
    from_up = shifted(rows, "shard", move(-1, 0))
    if side is not None:
        z_in, from_dn, from_up, side = lax.optimization_barrier((z_in, from_dn, from_up, side))
    z_from_dn = shifted(z_in, "shard", move(1, 0))
    z_from_up = shifted(z_in, "shard", move(-1, 0))
    far_a = shifted(from_dn[:half], "shard", move(1, 0))
    far_b = shifted(from_up[half:], "shard", move(-1, 0))
    z_far_a = shifted(z_from_dn[:half], "shard", move(1, 0))
    z_far_b = shifted(z_from_up[half:], "shard", move(-1, 0))
    blocks = [rows, z_in, from_dn, z_from_dn, from_up, z_from_up,
              jnp.concatenate([far_a, far_b]), jnp.concatenate([z_far_a, z_far_b])]
    s = lax.axis_index("shard")
    y, z = s // 2, s % 2
    sources = [
        s,
        y * 2 + (1 - z),
        ((y - 1) % ny) * 2 + z,
        ((y - 1) % ny) * 2 + (1 - z),
        ((y + 1) % ny) * 2 + z,
        ((y + 1) % ny) * 2 + (1 - z),
        ((y + 2) % ny) * 2 + z,
        ((y + 2) % ny) * 2 + (1 - z),
    ]
    return jnp.concatenate(blocks), sources, side


def gradient(activations, cotangents, k, c, side=None):
    tok_rows = activations[k, 0]
    cot_block = cotangents[k, 0]
    block, width = tok_rows.shape
    sub = width // (2 * CHUNKS)
    cols = tok_rows.reshape(block, 2, CHUNKS, sub)[:, :, c, :]
    gathered, sources, side = gather_tokens(cols, side)
    cot_rel = jnp.concatenate(
        [lax.dynamic_slice_in_dim(cot_block, src * block, block, axis=0) for src in sources]
    )
    d = lax.axis_index("dp")
    other = lax.dynamic_index_in_dim(gathered, 1 - d, axis=1, keepdims=False)
    mine = lax.dynamic_index_in_dim(gathered, d, axis=1, keepdims=False)
    dims = (((0,), (0,)), ((), ()))
    part_other = lax.dot_general(other, cot_rel, dims, preferred_element_type=jnp.float32)
    sent = lax.ppermute(part_other, "dp", [(0, 1), (1, 0)])
    part_mine = lax.dot_general(mine, cot_rel, dims, preferred_element_type=jnp.float32)
    return part_mine + sent, side


def x_hop(step):
    nx = 4

    def route_of(r):
        zh, x = divmod(r, nx)
        return zh * nx + (x + step) % nx
    return route_of


def trade_first(values):
    half = values.shape[0] // 2
    return (shifted(values[:half], "replica", x_hop(1)),
            shifted(values[half:], "replica", x_hop(-1)))


def trade_second(pair):
    a, b = pair
    return jnp.concatenate([shifted(a, "replica", x_hop(1)), shifted(b, "replica", x_hop(-1))])


def trade_with(level, values):
    if level == 1:
        return trade_second(trade_first(values))
    return swapped(values, "replica", level)


def trade_and_grad(level, stepped, activations, cotangents, k, c):
    if level == 1:
        grad, pair = gradient(activations, cotangents, k, c, trade_first(stepped))
        return trade_second(pair), grad
    return swapped(stepped, "replica", level), gradient(activations, cotangents, k, c)[0]


def stepped_of(grad, params_now, moment_now):
    moment_next = momentum_coef * moment_now + grad
    stepped = params_now - step_size * (grad + momentum_coef * moment_next)
    return stepped, moment_next


def local(round_index, activations, cotangents, params, momentum):
    rows = params.shape[1] // CHUNKS
    p_now = [params[0, c * rows:(c + 1) * rows] for c in range(CHUNKS)]
    m_now = [momentum[0, c * rows:(c + 1) * rows] for c in range(CHUNKS)]
    items = [(k, c) for k in range(ROUNDS) for c in range(CHUNKS)]
    grad = gradient(activations, cotangents, 0, 0)[0]
    for i, (k, c) in enumerate(items):
        stepped, m_now[c] = stepped_of(grad, p_now[c], m_now[c])
        level = round_index[k] % 3
        if i + 1 < len(items):
            k2, c2 = items[i + 1]
            branches = [partial(trade_and_grad, lv) for lv in range(3)]
            partner, grad = lax.switch(level, branches, stepped, activations, cotangents, k2, c2)
        else:
            branches = [partial(trade_with, lv) for lv in range(3)]
            partner = lax.switch(level, branches, stepped)
        p_now[c] = (stepped + partner) * 0.5
    return (jnp.concatenate(p_now)[None], jnp.concatenate(m_now)[None])


def solution(mesh):
    in_specs = (
        P(),
        P(None, "replica", ("dp", "shard"), None),
        P(None, "replica", "dp", "shard"),
        P("replica", "dp", "shard"),
        P("replica", "dp", "shard"),
    )
    out_specs = (P("replica", "dp", "shard"), P("replica", "dp", "shard"))
    return jax.shard_map(local, mesh=mesh, in_specs=in_specs, out_specs=out_specs, check_vma=False)
```

```python
from functools import partial

import jax
import jax.numpy as jnp
from jax import lax
from jax.sharding import PartitionSpec as P

ROUNDS = 2


momentum_coef = 0.9
step_size = 0.25


def swapped(block, axis, stride):
    count = lax.axis_size(axis)
    route = []
    for low in range(count):
        high = low | 1 << stride
        if high != low and high < count:
            route += [(low, high), (high, low)]
    return lax.ppermute(block, axis, route)


def shifted(block, axis, route_of):
    count = lax.axis_size(axis)
    return lax.ppermute(block, axis, [(i, route_of(i)) for i in range(count)])


def gather_tokens(rows, side=None, advance=None):
    count = lax.axis_size("shard")
    ny = count // 2
    half = rows.shape[0] // 2

    def move(y_step, z_flip):
        def route_of(s):
            y, z = divmod(s, 2)
            return ((y + y_step) % ny) * 2 + (z ^ z_flip)
        return route_of

    z_in = shifted(rows, "shard", move(0, 1))
    from_dn = shifted(rows, "shard", move(1, 0))
    from_up = shifted(rows, "shard", move(-1, 0))
    if side is not None:
        z_in, from_dn, from_up, side = lax.optimization_barrier((z_in, from_dn, from_up, side))
        side = advance(side)
    z_from_dn = shifted(z_in, "shard", move(1, 0))
    z_from_up = shifted(z_in, "shard", move(-1, 0))
    if side is not None:
        z_from_dn, z_from_up, side = lax.optimization_barrier((z_from_dn, z_from_up, side))
    far_a = shifted(from_dn[:half], "shard", move(1, 0))
    far_b = shifted(from_up[half:], "shard", move(-1, 0))
    z_far_a = shifted(z_from_dn[:half], "shard", move(1, 0))
    z_far_b = shifted(z_from_up[half:], "shard", move(-1, 0))
    blocks = [rows, z_in, from_dn, z_from_dn, from_up, z_from_up,
              jnp.concatenate([far_a, far_b]), jnp.concatenate([z_far_a, z_far_b])]
    s = lax.axis_index("shard")
    y, z = s // 2, s % 2
    sources = [
        s,
        y * 2 + (1 - z),
        ((y - 1) % ny) * 2 + z,
        ((y - 1) % ny) * 2 + (1 - z),
        ((y + 1) % ny) * 2 + z,
        ((y + 1) % ny) * 2 + (1 - z),
        ((y + 2) % ny) * 2 + z,
        ((y + 2) % ny) * 2 + (1 - z),
    ]
    return jnp.concatenate(blocks), sources, side


def gradient(activations, cotangents, k, side=None, advance=None):
    tok_rows = activations[k, 0]
    cot_block = cotangents[k, 0]
    block = tok_rows.shape[0]
    gathered, sources, side = gather_tokens(tok_rows, side, advance)
    cot_rel = jnp.concatenate(
        [lax.dynamic_slice_in_dim(cot_block, src * block, block, axis=0) for src in sources]
    )
    d = lax.axis_index("dp")
    n_rows = tok_rows.shape[1] // 2
    other = lax.dynamic_slice_in_dim(gathered, (1 - d) * n_rows, n_rows, axis=1)
    mine = lax.dynamic_slice_in_dim(gathered, d * n_rows, n_rows, axis=1)
    dims = (((0,), (0,)), ((), ()))
    part_other = lax.dot_general(other, cot_rel, dims, preferred_element_type=jnp.float32)
    sent = lax.ppermute(part_other, "dp", [(0, 1), (1, 0)])
    part_mine = lax.dot_general(mine, cot_rel, dims, preferred_element_type=jnp.float32)
    return part_mine + sent, side


def x_hop(step):
    nx = 4

    def route_of(r):
        zh, x = divmod(r, nx)
        return zh * nx + (x + step) % nx
    return route_of


def trade_first(values):
    half = values.shape[0] // 2
    return (shifted(values[:half], "replica", x_hop(1)),
            shifted(values[half:], "replica", x_hop(-1)))


def trade_second(pair):
    a, b = pair
    return jnp.concatenate([shifted(a, "replica", x_hop(1)), shifted(b, "replica", x_hop(-1))])


def trade_with(level, values):
    if level == 1:
        return trade_second(trade_first(values))
    return swapped(values, "replica", level)


def stepped_of(grad, params_now, moment_now):
    moment_next = momentum_coef * moment_now + grad
    stepped = params_now - step_size * (grad + momentum_coef * moment_next)
    return stepped, moment_next


def trade_and_grad(level, stepped, activations, cotangents, k):
    if level == 1:
        grad, partner = gradient(activations, cotangents, k, trade_first(stepped), trade_second)
        return partner, grad
    return swapped(stepped, "replica", level), gradient(activations, cotangents, k)[0]


def local(round_index, activations, cotangents, params, momentum):
    params_now = params[0]
    moment_now = momentum[0]
    grad = gradient(activations, cotangents, 0)[0]
    for k in range(ROUNDS):
        stepped, moment_now = stepped_of(grad, params_now, moment_now)
        level = round_index[k] % 3
        if k + 1 < ROUNDS:
            branches = [partial(trade_and_grad, lv) for lv in range(3)]
            partner, grad = lax.switch(level, branches, stepped, activations, cotangents, k + 1)
        else:
            branches = [partial(trade_with, lv) for lv in range(3)]
            partner = lax.switch(level, branches, stepped)
        params_now = (stepped + partner) * 0.5
    return (params_now[None], moment_now[None])


def solution(mesh):
    in_specs = (
        P(),
        P(None, "replica", ("dp", "shard"), None),
        P(None, "replica", "dp", "shard"),
        P("replica", "dp", "shard"),
        P("replica", "dp", "shard"),
    )
    out_specs = (P("replica", "dp", "shard"), P("replica", "dp", "shard"))
    return jax.shard_map(local, mesh=mesh, in_specs=in_specs, out_specs=out_specs, check_vma=False)
```

```python
from functools import partial

import jax
import jax.numpy as jnp
from jax import lax
from jax.sharding import PartitionSpec as P

ROUNDS = 2


momentum_coef = 0.9
step_size = 0.25


def swapped(block, axis, stride):
    count = lax.axis_size(axis)
    route = []
    for low in range(count):
        high = low | 1 << stride
        if high != low and high < count:
            route += [(low, high), (high, low)]
    return lax.ppermute(block, axis, route)


def shifted(block, axis, route_of):
    count = lax.axis_size(axis)
    return lax.ppermute(block, axis, [(i, route_of(i)) for i in range(count)])


def gather_tokens(rows, side=None, advance=None):
    count = lax.axis_size("shard")
    ny = count // 2
    half = rows.shape[0] // 2

    def move(y_step, z_flip):
        def route_of(s):
            y, z = divmod(s, 2)
            return ((y + y_step) % ny) * 2 + (z ^ z_flip)
        return route_of

    z_in = shifted(rows, "shard", move(0, 1))
    from_dn = shifted(rows, "shard", move(1, 0))
    from_up = shifted(rows, "shard", move(-1, 0))
    if side is not None:
        z_in, from_dn, from_up, side = lax.optimization_barrier((z_in, from_dn, from_up, side))
        side = advance(side)
    z_from_dn = shifted(z_in, "shard", move(1, 0))
    z_from_up = shifted(z_in, "shard", move(-1, 0))
    if side is not None:
        z_from_dn, z_from_up, side = lax.optimization_barrier((z_from_dn, z_from_up, side))
    far_a = shifted(from_dn[:half], "shard", move(1, 0))
    far_b = shifted(from_up[half:], "shard", move(-1, 0))
    z_far_a = shifted(z_from_dn[:half], "shard", move(1, 0))
    z_far_b = shifted(z_from_up[half:], "shard", move(-1, 0))
    blocks = [rows, z_in, from_dn, z_from_dn, from_up, z_from_up,
              jnp.concatenate([far_a, far_b]), jnp.concatenate([z_far_a, z_far_b])]
    s = lax.axis_index("shard")
    y, z = s // 2, s % 2
    sources = [
        s,
        y * 2 + (1 - z),
        ((y - 1) % ny) * 2 + z,
        ((y - 1) % ny) * 2 + (1 - z),
        ((y + 1) % ny) * 2 + z,
        ((y + 1) % ny) * 2 + (1 - z),
        ((y + 2) % ny) * 2 + z,
        ((y + 2) % ny) * 2 + (1 - z),
    ]
    return jnp.concatenate(blocks), sources, side


def gradient(activations, cotangents, k, side=None, advance=None):
    tok_rows = activations[k, 0]
    cot_block = cotangents[k, 0]
    block = tok_rows.shape[0]
    gathered, sources, side = gather_tokens(tok_rows, side, advance)
    cot_rel = jnp.concatenate(
        [lax.dynamic_slice_in_dim(cot_block, src * block, block, axis=0) for src in sources]
    )
    d = lax.axis_index("dp")
    n_rows = tok_rows.shape[1] // 2
    other = lax.dynamic_slice_in_dim(gathered, (1 - d) * n_rows, n_rows, axis=1)
    mine = lax.dynamic_slice_in_dim(gathered, d * n_rows, n_rows, axis=1)
    dims = (((0,), (0,)), ((), ()))
    part_other = lax.dot_general(other, cot_rel, dims, preferred_element_type=jnp.float32)
    sent = lax.ppermute(part_other, "dp", [(0, 1), (1, 0)])
    part_mine = lax.optimization_barrier(
        lax.dot_general(mine, cot_rel, dims, preferred_element_type=jnp.float32))
    return part_mine + sent, side


def x_hop(step):
    nx = 4

    def route_of(r):
        zh, x = divmod(r, nx)
        return zh * nx + (x + step) % nx
    return route_of


def trade_first(values):
    half = values.shape[0] // 2
    return (shifted(values[:half], "replica", x_hop(1)),
            shifted(values[half:], "replica", x_hop(-1)))


def trade_second(pair):
    a, b = pair
    return jnp.concatenate([shifted(a, "replica", x_hop(1)), shifted(b, "replica", x_hop(-1))])


def trade_with(level, values):
    if level == 1:
        return trade_second(trade_first(values))
    return swapped(values, "replica", level)


def stepped_of(grad, params_now, moment_now):
    moment_next = momentum_coef * moment_now + grad
    stepped = params_now - step_size * (grad + momentum_coef * moment_next)
    return stepped, moment_next


def trade_and_grad(level, stepped, activations, cotangents, k):
    if level == 1:
        grad, partner = gradient(activations, cotangents, k, trade_first(stepped), trade_second)
        return partner, grad
    return swapped(stepped, "replica", level), gradient(activations, cotangents, k)[0]


def local(round_index, activations, cotangents, params, momentum):
    params_now = params[0]
    moment_now = momentum[0]
    grad = gradient(activations, cotangents, 0)[0]
    for k in range(ROUNDS):
        stepped, moment_now = stepped_of(grad, params_now, moment_now)
        level = round_index[k] % 3
        if k + 1 < ROUNDS:
            branches = [partial(trade_and_grad, lv) for lv in range(3)]
            partner, grad = lax.switch(level, branches, stepped, activations, cotangents, k + 1)
        else:
            branches = [partial(trade_with, lv) for lv in range(3)]
            partner = lax.switch(level, branches, stepped)
        params_now = (stepped + partner) * 0.5
    return (params_now[None], moment_now[None])


def solution(mesh):
    in_specs = (
        P(),
        P(None, "replica", ("dp", "shard"), None),
        P(None, "replica", "dp", "shard"),
        P("replica", "dp", "shard"),
        P("replica", "dp", "shard"),
    )
    out_specs = (P("replica", "dp", "shard"), P("replica", "dp", "shard"))
    return jax.shard_map(local, mesh=mesh, in_specs=in_specs, out_specs=out_specs, check_vma=False)
```

```python
from functools import partial

import jax
import jax.numpy as jnp
from jax import lax
from jax.sharding import PartitionSpec as P

ROUNDS = 2


momentum_coef = 0.9
step_size = 0.25


def swapped(block, axis, stride):
    count = lax.axis_size(axis)
    route = []
    for low in range(count):
        high = low | 1 << stride
        if high != low and high < count:
            route += [(low, high), (high, low)]
    return lax.ppermute(block, axis, route)


def shifted(block, axis, route_of):
    count = lax.axis_size(axis)
    return lax.ppermute(block, axis, [(i, route_of(i)) for i in range(count)])


def gather_tokens(rows, side=None, advance=None):
    count = lax.axis_size("shard")
    ny = count // 2
    half = rows.shape[0] // 2

    def move(y_step, z_flip):
        def route_of(s):
            y, z = divmod(s, 2)
            return ((y + y_step) % ny) * 2 + (z ^ z_flip)
        return route_of

    z_in = shifted(rows, "shard", move(0, 1))
    from_dn = shifted(rows, "shard", move(1, 0))
    from_up = shifted(rows, "shard", move(-1, 0))
    if side is not None:
        z_in, from_dn, from_up, side = lax.optimization_barrier((z_in, from_dn, from_up, side))
        side = advance(side)
    far_a = shifted(from_dn[:half], "shard", move(1, 0))
    far_b = shifted(from_up[half:], "shard", move(-1, 0))
    far_a, far_b, z_in = lax.optimization_barrier((far_a, far_b, z_in))
    far = jnp.concatenate([far_a, far_b])
    z_far = shifted(far, "shard", move(0, 1))
    z_from_dn = shifted(z_in, "shard", move(1, 0))
    z_from_up = shifted(z_in, "shard", move(-1, 0))
    if side is not None:
        z_from_dn, z_from_up, side = lax.optimization_barrier((z_from_dn, z_from_up, side))
    blocks = [rows, z_in, from_dn, z_from_dn, from_up, z_from_up, far, z_far]
    s = lax.axis_index("shard")
    y, z = s // 2, s % 2
    sources = [
        s,
        y * 2 + (1 - z),
        ((y - 1) % ny) * 2 + z,
        ((y - 1) % ny) * 2 + (1 - z),
        ((y + 1) % ny) * 2 + z,
        ((y + 1) % ny) * 2 + (1 - z),
        ((y + 2) % ny) * 2 + z,
        ((y + 2) % ny) * 2 + (1 - z),
    ]
    return jnp.concatenate(blocks), sources, side


def gradient(activations, cotangents, k, side=None, advance=None):
    tok_rows = activations[k, 0]
    cot_block = cotangents[k, 0]
    block = tok_rows.shape[0]
    gathered, sources, side = gather_tokens(tok_rows, side, advance)
    cot_rel = jnp.concatenate(
        [lax.dynamic_slice_in_dim(cot_block, src * block, block, axis=0) for src in sources]
    )
    d = lax.axis_index("dp")
    n_rows = tok_rows.shape[1] // 2
    other = lax.dynamic_slice_in_dim(gathered, (1 - d) * n_rows, n_rows, axis=1)
    mine = lax.dynamic_slice_in_dim(gathered, d * n_rows, n_rows, axis=1)
    dims = (((0,), (0,)), ((), ()))
    part_other = lax.dot_general(other, cot_rel, dims, preferred_element_type=jnp.float32)
    sent = lax.ppermute(part_other, "dp", [(0, 1), (1, 0)])
    part_mine = lax.optimization_barrier(
        lax.dot_general(mine, cot_rel, dims, preferred_element_type=jnp.float32))
    return part_mine + sent, side


def x_hop(step):
    nx = 4

    def route_of(r):
        zh, x = divmod(r, nx)
        return zh * nx + (x + step) % nx
    return route_of


def trade_first(values):
    half = values.shape[0] // 2
    return (shifted(values[:half], "replica", x_hop(1)),
            shifted(values[half:], "replica", x_hop(-1)))


def trade_second(pair):
    a, b = pair
    return jnp.concatenate([shifted(a, "replica", x_hop(1)), shifted(b, "replica", x_hop(-1))])


def trade_with(level, values):
    if level == 1:
        return trade_second(trade_first(values))
    return swapped(values, "replica", level)


def stepped_of(grad, params_now, moment_now):
    moment_next = momentum_coef * moment_now + grad
    stepped = params_now - step_size * (grad + momentum_coef * moment_next)
    return stepped, moment_next


def trade_and_grad(level, stepped, activations, cotangents, k):
    if level == 1:
        grad, partner = gradient(activations, cotangents, k, trade_first(stepped), trade_second)
        return partner, grad
    return swapped(stepped, "replica", level), gradient(activations, cotangents, k)[0]


def local(round_index, activations, cotangents, params, momentum):
    params_now = params[0]
    moment_now = momentum[0]
    grad = gradient(activations, cotangents, 0)[0]
    for k in range(ROUNDS):
        stepped, moment_now = stepped_of(grad, params_now, moment_now)
        level = round_index[k] % 3
        if k + 1 < ROUNDS:
            branches = [partial(trade_and_grad, lv) for lv in range(3)]
            partner, grad = lax.switch(level, branches, stepped, activations, cotangents, k + 1)
        else:
            branches = [partial(trade_with, lv) for lv in range(3)]
            partner = lax.switch(level, branches, stepped)
        params_now = (stepped + partner) * 0.5
    return (params_now[None], moment_now[None])


def solution(mesh):
    in_specs = (
        P(),
        P(None, "replica", ("dp", "shard"), None),
        P(None, "replica", "dp", "shard"),
        P("replica", "dp", "shard"),
        P("replica", "dp", "shard"),
    )
    out_specs = (P("replica", "dp", "shard"), P("replica", "dp", "shard"))
    return jax.shard_map(local, mesh=mesh, in_specs=in_specs, out_specs=out_specs, check_vma=False)
```

```python
from functools import partial

import jax
import jax.numpy as jnp
from jax import lax
from jax.sharding import PartitionSpec as P

ROUNDS = 2


momentum_coef = 0.9
step_size = 0.25


def swapped(block, axis, stride):
    count = lax.axis_size(axis)
    route = []
    for low in range(count):
        high = low | 1 << stride
        if high != low and high < count:
            route += [(low, high), (high, low)]
    return lax.ppermute(block, axis, route)


def shifted(block, axis, route_of):
    count = lax.axis_size(axis)
    return lax.ppermute(block, axis, [(i, route_of(i)) for i in range(count)])


def gather_tokens(rows, first, side=None, advance=None):
    count = lax.axis_size("shard")
    ny = count // 2
    half = rows.shape[0] // 2

    def move(y_step, z_flip):
        def route_of(s):
            y, z = divmod(s, 2)
            return ((y + y_step) % ny) * 2 + (z ^ z_flip)
        return route_of

    z_in = shifted(rows, "shard", move(0, 1))
    from_dn = shifted(rows, "shard", move(1, 0))
    from_up = shifted(rows, "shard", move(-1, 0))
    if side is not None:
        z_in, from_dn, from_up, side = lax.optimization_barrier((z_in, from_dn, from_up, side))
        side = advance(side)
    far_a = shifted(from_dn[:half], "shard", move(1, 0))
    far_b = shifted(from_up[half:], "shard", move(-1, 0))
    s = lax.axis_index("shard")
    y, z = s // 2, s % 2
    done = first([(rows, s), (z_in, y * 2 + (1 - z)), (from_dn, ((y - 1) % ny) * 2 + z),
                  (from_up, ((y + 1) % ny) * 2 + z)])
    far_a, far_b, z_in, done = lax.optimization_barrier((far_a, far_b, z_in, done))
    far = jnp.concatenate([far_a, far_b])
    z_far = shifted(far, "shard", move(0, 1))
    z_from_dn = shifted(z_in, "shard", move(1, 0))
    z_from_up = shifted(z_in, "shard", move(-1, 0))
    if side is not None:
        z_from_dn, z_from_up, side = lax.optimization_barrier((z_from_dn, z_from_up, side))
    late = [(far, ((y + 2) % ny) * 2 + z), (z_from_dn, ((y - 1) % ny) * 2 + (1 - z)),
            (z_from_up, ((y + 1) % ny) * 2 + (1 - z)), (z_far, ((y + 2) % ny) * 2 + (1 - z))]
    return done, late, side


def gradient(activations, cotangents, k, side=None, advance=None):
    tok_rows = activations[k, 0]
    cot_block = cotangents[k, 0]
    block = tok_rows.shape[0]
    d = lax.axis_index("dp")
    n_rows = tok_rows.shape[1] // 2
    dims = (((0,), (0,)), ((), ()))

    def partials(group):
        gathered = jnp.concatenate([blk for blk, _ in group])
        cot_rel = jnp.concatenate(
            [lax.dynamic_slice_in_dim(cot_block, src * block, block, axis=0) for _, src in group]
        )
        other = lax.dynamic_slice_in_dim(gathered, (1 - d) * n_rows, n_rows, axis=1)
        mine = lax.dynamic_slice_in_dim(gathered, d * n_rows, n_rows, axis=1)
        return (lax.dot_general(other, cot_rel, dims, preferred_element_type=jnp.float32),
                lax.dot_general(mine, cot_rel, dims, preferred_element_type=jnp.float32))

    (other_early, mine_early), late, side = gather_tokens(tok_rows, partials, side, advance)
    other_late, mine_late = partials(late)
    part_other = other_early + other_late
    sent = lax.ppermute(part_other, "dp", [(0, 1), (1, 0)])
    part_mine = lax.optimization_barrier(mine_early + mine_late)
    return part_mine + sent, side


def x_hop(step):
    nx = 4

    def route_of(r):
        zh, x = divmod(r, nx)
        return zh * nx + (x + step) % nx
    return route_of


def trade_first(values):
    half = values.shape[0] // 2
    return (shifted(values[:half], "replica", x_hop(1)),
            shifted(values[half:], "replica", x_hop(-1)))


def trade_second(pair):
    a, b = pair
    return jnp.concatenate([shifted(a, "replica", x_hop(1)), shifted(b, "replica", x_hop(-1))])


def trade_with(level, values):
    if level == 1:
        return trade_second(trade_first(values))
    return swapped(values, "replica", level)


def stepped_of(grad, params_now, moment_now):
    moment_next = momentum_coef * moment_now + grad
    stepped = params_now - step_size * (grad + momentum_coef * moment_next)
    return stepped, moment_next


def trade_and_grad(level, stepped, activations, cotangents, k):
    if level == 1:
        grad, partner = gradient(activations, cotangents, k, trade_first(stepped), trade_second)
        return partner, grad
    return swapped(stepped, "replica", level), gradient(activations, cotangents, k)[0]


def local(round_index, activations, cotangents, params, momentum):
    params_now = params[0]
    moment_now = momentum[0]
    grad = gradient(activations, cotangents, 0)[0]
    for k in range(ROUNDS):
        stepped, moment_now = stepped_of(grad, params_now, moment_now)
        level = round_index[k] % 3
        if k + 1 < ROUNDS:
            branches = [partial(trade_and_grad, lv) for lv in range(3)]
            partner, grad = lax.switch(level, branches, stepped, activations, cotangents, k + 1)
        else:
            branches = [partial(trade_with, lv) for lv in range(3)]
            partner = lax.switch(level, branches, stepped)
        params_now = (stepped + partner) * 0.5
    return (params_now[None], moment_now[None])


def solution(mesh):
    in_specs = (
        P(),
        P(None, "replica", ("dp", "shard"), None),
        P(None, "replica", "dp", "shard"),
        P("replica", "dp", "shard"),
        P("replica", "dp", "shard"),
    )
    out_specs = (P("replica", "dp", "shard"), P("replica", "dp", "shard"))
    return jax.shard_map(local, mesh=mesh, in_specs=in_specs, out_specs=out_specs, check_vma=False)
```

```python
from functools import partial

import jax
import jax.numpy as jnp
from jax import lax
from jax.sharding import PartitionSpec as P

ROUNDS = 2


momentum_coef = 0.9
step_size = 0.25


def swapped(block, axis, stride):
    count = lax.axis_size(axis)
    route = []
    for low in range(count):
        high = low | 1 << stride
        if high != low and high < count:
            route += [(low, high), (high, low)]
    return lax.ppermute(block, axis, route)


def shifted(block, axis, route_of):
    count = lax.axis_size(axis)
    return lax.ppermute(block, axis, [(i, route_of(i)) for i in range(count)])


def gather_tokens(rows, first, side=None, advance=None, z_light=False):
    count = lax.axis_size("shard")
    ny = count // 2
    half = rows.shape[0] // 2

    def move(y_step, z_flip):
        def route_of(s):
            y, z = divmod(s, 2)
            return ((y + y_step) % ny) * 2 + (z ^ z_flip)
        return route_of

    z_in = shifted(rows, "shard", move(0, 1))
    from_dn = shifted(rows, "shard", move(1, 0))
    from_up = shifted(rows, "shard", move(-1, 0))
    if side is not None:
        z_in, from_dn, from_up, side = lax.optimization_barrier((z_in, from_dn, from_up, side))
        side = advance(side)
    far_a = shifted(from_dn[:half], "shard", move(1, 0))
    far_b = shifted(from_up[half:], "shard", move(-1, 0))
    s = lax.axis_index("shard")
    y, z = s // 2, s % 2
    done = first([(rows, s), (z_in, y * 2 + (1 - z)), (from_dn, ((y - 1) % ny) * 2 + z),
                  (from_up, ((y + 1) % ny) * 2 + z)])
    far_a, far_b, z_in, done = lax.optimization_barrier((far_a, far_b, z_in, done))
    far = jnp.concatenate([far_a, far_b])
    if not z_light:
        z_far = shifted(far, "shard", move(0, 1))
    z_from_dn = shifted(z_in, "shard", move(1, 0))
    z_from_up = shifted(z_in, "shard", move(-1, 0))
    if z_light:
        z_far = jnp.concatenate([shifted(z_from_dn[:half], "shard", move(1, 0)),
                                 shifted(z_from_up[half:], "shard", move(-1, 0))])
    if side is not None:
        z_from_dn, z_from_up, side = lax.optimization_barrier((z_from_dn, z_from_up, side))
    late = [(far, ((y + 2) % ny) * 2 + z), (z_from_dn, ((y - 1) % ny) * 2 + (1 - z)),
            (z_from_up, ((y + 1) % ny) * 2 + (1 - z)), (z_far, ((y + 2) % ny) * 2 + (1 - z))]
    return done, late, side


def gradient(activations, cotangents, k, side=None, advance=None, z_light=False):
    tok_rows = activations[k, 0]
    cot_block = cotangents[k, 0]
    block = tok_rows.shape[0]
    d = lax.axis_index("dp")
    n_rows = tok_rows.shape[1] // 2
    dims = (((0,), (0,)), ((), ()))

    def partials(group):
        gathered = jnp.concatenate([blk for blk, _ in group])
        cot_rel = jnp.concatenate(
            [lax.dynamic_slice_in_dim(cot_block, src * block, block, axis=0) for _, src in group]
        )
        other = lax.dynamic_slice_in_dim(gathered, (1 - d) * n_rows, n_rows, axis=1)
        mine = lax.dynamic_slice_in_dim(gathered, d * n_rows, n_rows, axis=1)
        return (lax.dot_general(other, cot_rel, dims, preferred_element_type=jnp.float32),
                lax.dot_general(mine, cot_rel, dims, preferred_element_type=jnp.float32))

    (other_early, mine_early), late, side = gather_tokens(tok_rows, partials, side, advance, z_light)
    other_late, mine_late = partials(late)
    part_other = other_early + other_late
    sent = lax.ppermute(part_other, "dp", [(0, 1), (1, 0)])
    part_mine = lax.optimization_barrier(mine_early + mine_late)
    return part_mine + sent, side


def x_hop(step):
    nx = 4

    def route_of(r):
        zh, x = divmod(r, nx)
        return zh * nx + (x + step) % nx
    return route_of


def trade_first(values):
    half = values.shape[0] // 2
    return (shifted(values[:half], "replica", x_hop(1)),
            shifted(values[half:], "replica", x_hop(-1)))


def trade_second(pair):
    a, b = pair
    return jnp.concatenate([shifted(a, "replica", x_hop(1)), shifted(b, "replica", x_hop(-1))])


def trade_with(level, values):
    if level == 1:
        return trade_second(trade_first(values))
    return swapped(values, "replica", level)


def stepped_of(grad, params_now, moment_now):
    moment_next = momentum_coef * moment_now + grad
    stepped = params_now - step_size * (grad + momentum_coef * moment_next)
    return stepped, moment_next


def trade_and_grad(level, stepped, activations, cotangents, k):
    if level == 1:
        grad, partner = gradient(activations, cotangents, k, trade_first(stepped), trade_second)
        return partner, grad
    return (swapped(stepped, "replica", level),
            gradient(activations, cotangents, k, z_light=level == 2)[0])


def local(round_index, activations, cotangents, params, momentum):
    params_now = params[0]
    moment_now = momentum[0]
    grad = gradient(activations, cotangents, 0)[0]
    for k in range(ROUNDS):
        stepped, moment_now = stepped_of(grad, params_now, moment_now)
        level = round_index[k] % 3
        if k + 1 < ROUNDS:
            branches = [partial(trade_and_grad, lv) for lv in range(3)]
            partner, grad = lax.switch(level, branches, stepped, activations, cotangents, k + 1)
        else:
            branches = [partial(trade_with, lv) for lv in range(3)]
            partner = lax.switch(level, branches, stepped)
        params_now = (stepped + partner) * 0.5
    return (params_now[None], moment_now[None])


def solution(mesh):
    in_specs = (
        P(),
        P(None, "replica", ("dp", "shard"), None),
        P(None, "replica", "dp", "shard"),
        P("replica", "dp", "shard"),
        P("replica", "dp", "shard"),
    )
    out_specs = (P("replica", "dp", "shard"), P("replica", "dp", "shard"))
    return jax.shard_map(local, mesh=mesh, in_specs=in_specs, out_specs=out_specs, check_vma=False)
```

```python
from functools import partial

import jax
import jax.numpy as jnp
from jax import lax
from jax.sharding import PartitionSpec as P

ROUNDS = 2


momentum_coef = 0.9
step_size = 0.25


def swapped(block, axis, stride):
    count = lax.axis_size(axis)
    route = []
    for low in range(count):
        high = low | 1 << stride
        if high != low and high < count:
            route += [(low, high), (high, low)]
    return lax.ppermute(block, axis, route)


def shifted(block, axis, route_of):
    count = lax.axis_size(axis)
    return lax.ppermute(block, axis, [(i, route_of(i)) for i in range(count)])


def gather_tokens(rows, first, side=None, advance=None, z_light=False):
    count = lax.axis_size("shard")
    ny = count // 2
    half = rows.shape[0] // 2

    def move(y_step, z_flip):
        def route_of(s):
            y, z = divmod(s, 2)
            return ((y + y_step) % ny) * 2 + (z ^ z_flip)
        return route_of

    z_in = shifted(rows, "shard", move(0, 1))
    from_dn = shifted(rows, "shard", move(1, 0))
    from_up = shifted(rows, "shard", move(-1, 0))
    if side is not None:
        z_in, from_dn, from_up, side = lax.optimization_barrier((z_in, from_dn, from_up, side))
        side = advance(side)
    far_a = shifted(from_dn[:half], "shard", move(1, 0))
    far_b = shifted(from_up[half:], "shard", move(-1, 0))
    s = lax.axis_index("shard")
    y, z = s // 2, s % 2
    done = first([(rows, s), (z_in, y * 2 + (1 - z)), (from_dn, ((y - 1) % ny) * 2 + z),
                  (from_up, ((y + 1) % ny) * 2 + z)])
    far_a, far_b, z_in, done = lax.optimization_barrier((far_a, far_b, z_in, done))
    far = jnp.concatenate([far_a, far_b])
    if not z_light:
        z_far = shifted(far, "shard", move(0, 1))
    z_from_dn = shifted(z_in, "shard", move(1, 0))
    z_from_up = shifted(z_in, "shard", move(-1, 0))
    if z_light:
        z_far = jnp.concatenate([shifted(z_from_dn[:half], "shard", move(1, 0)),
                                 shifted(z_from_up[half:], "shard", move(-1, 0))])
    if side is not None:
        z_from_dn, z_from_up, side = lax.optimization_barrier((z_from_dn, z_from_up, side))
    late = [(far, ((y + 2) % ny) * 2 + z), (z_from_dn, ((y - 1) % ny) * 2 + (1 - z)),
            (z_from_up, ((y + 1) % ny) * 2 + (1 - z)), (z_far, ((y + 2) % ny) * 2 + (1 - z))]
    return done, late, side


def gradient(activations, cotangents, k, side=None, advance=None, z_light=False):
    tok_rows = activations[k, 0]
    cot_block = cotangents[k, 0]
    block = tok_rows.shape[0]
    d = lax.axis_index("dp")
    n_rows = tok_rows.shape[1] // 2
    dims = (((0,), (0,)), ((), ()))

    def partials(group):
        gathered = jnp.concatenate([blk for blk, _ in group])
        cot_rel = jnp.concatenate(
            [lax.dynamic_slice_in_dim(cot_block, src * block, block, axis=0) for _, src in group]
        )
        other = lax.dynamic_slice_in_dim(gathered, (1 - d) * n_rows, n_rows, axis=1)
        mine = lax.dynamic_slice_in_dim(gathered, d * n_rows, n_rows, axis=1)
        return (lax.dot_general(other, cot_rel, dims, preferred_element_type=jnp.float32),
                lax.dot_general(mine, cot_rel, dims, preferred_element_type=jnp.float32))

    (other_early, mine_early), late, side = gather_tokens(tok_rows, partials, side, advance, z_light)
    other_late, mine_late = partials(late)
    part_other = other_early + other_late
    sent = lax.ppermute(part_other, "dp", [(0, 1), (1, 0)])
    part_mine = lax.optimization_barrier(mine_early + mine_late)
    return part_mine + sent, side


def x_hop(step):
    nx = 4

    def route_of(r):
        zh, x = divmod(r, nx)
        return zh * nx + (x + step) % nx
    return route_of


def trade_first(values):
    half = values.shape[0] // 2
    return (shifted(values[:half], "replica", x_hop(1)),
            shifted(values[half:], "replica", x_hop(-1)))


def trade_second(pair):
    a, b = pair
    return jnp.concatenate([shifted(a, "replica", x_hop(1)), shifted(b, "replica", x_hop(-1))])


def trade_with(level, values):
    if level == 1:
        return trade_second(trade_first(values))
    return swapped(values, "replica", level)


def trade_and_grad(level, stepped, moment, activations, cotangents, k):
    if level == 1:
        grad, partner = gradient(activations, cotangents, k, trade_first(stepped), trade_second)
    else:
        partner = swapped(stepped, "replica", level)
        grad = gradient(activations, cotangents, k, z_light=level == 2)[0]
    return base_of((stepped + partner) * 0.5, moment), grad


moment_part = step_size * momentum_coef * momentum_coef
grad_part = step_size * (1 + momentum_coef)


def base_of(params_now, moment_now):
    return params_now - moment_part * moment_now


def local(round_index, activations, cotangents, params, momentum):
    moment_now = momentum[0]
    base = lax.optimization_barrier(base_of(params[0], moment_now))
    grad = gradient(activations, cotangents, 0)[0]
    for k in range(ROUNDS):
        stepped = base - grad_part * grad
        moment_now = momentum_coef * moment_now + grad
        level = round_index[k] % 3
        if k + 1 < ROUNDS:
            branches = [partial(trade_and_grad, lv) for lv in range(3)]
            base, grad = lax.switch(level, branches, stepped, moment_now, activations, cotangents, k + 1)
        else:
            branches = [partial(trade_with, lv) for lv in range(3)]
            partner = lax.switch(level, branches, stepped)
            params_now = (stepped + partner) * 0.5
    return (params_now[None], moment_now[None])


def solution(mesh):
    in_specs = (
        P(),
        P(None, "replica", ("dp", "shard"), None),
        P(None, "replica", "dp", "shard"),
        P("replica", "dp", "shard"),
        P("replica", "dp", "shard"),
    )
    out_specs = (P("replica", "dp", "shard"), P("replica", "dp", "shard"))
    return jax.shard_map(local, mesh=mesh, in_specs=in_specs, out_specs=out_specs, check_vma=False)
```

```python
from functools import partial

import jax
import jax.numpy as jnp
from jax import lax
from jax.sharding import PartitionSpec as P

ROUNDS = 2


momentum_coef = 0.9
step_size = 0.25


def swapped(block, axis, stride):
    count = lax.axis_size(axis)
    route = []
    for low in range(count):
        high = low | 1 << stride
        if high != low and high < count:
            route += [(low, high), (high, low)]
    return lax.ppermute(block, axis, route)


def shifted(block, axis, route_of):
    count = lax.axis_size(axis)
    return lax.ppermute(block, axis, [(i, route_of(i)) for i in range(count)])


def gather_tokens(rows, first, side=None, advance=None, z_light=False):
    count = lax.axis_size("shard")
    ny = count // 2
    half = rows.shape[0] // 2

    def move(y_step, z_flip):
        def route_of(s):
            y, z = divmod(s, 2)
            return ((y + y_step) % ny) * 2 + (z ^ z_flip)
        return route_of

    z_in = shifted(rows, "shard", move(0, 1))
    from_dn = shifted(rows, "shard", move(1, 0))
    from_up = shifted(rows, "shard", move(-1, 0))
    if side is not None:
        z_in, from_dn, from_up, side = lax.optimization_barrier((z_in, from_dn, from_up, side))
        side = advance(side)
    far_a = shifted(from_dn[:half], "shard", move(1, 0))
    far_b = shifted(from_up[half:], "shard", move(-1, 0))
    s = lax.axis_index("shard")
    y, z = s // 2, s % 2
    done = first([(rows, s), (z_in, y * 2 + (1 - z)), (from_dn, ((y - 1) % ny) * 2 + z),
                  (from_up, ((y + 1) % ny) * 2 + z)])
    far_a, far_b, z_in, done = lax.optimization_barrier((far_a, far_b, z_in, done))
    far = jnp.concatenate([far_a, far_b])
    if not z_light:
        z_far = shifted(far, "shard", move(0, 1))
    z_from_dn = shifted(z_in, "shard", move(1, 0))
    z_from_up = shifted(z_in, "shard", move(-1, 0))
    if z_light:
        z_far = jnp.concatenate([shifted(z_from_dn[:half], "shard", move(1, 0)),
                                 shifted(z_from_up[half:], "shard", move(-1, 0))])
    if side is not None:
        z_from_dn, z_from_up, side = lax.optimization_barrier((z_from_dn, z_from_up, side))
    late = [(far, ((y + 2) % ny) * 2 + z), (z_from_dn, ((y - 1) % ny) * 2 + (1 - z)),
            (z_from_up, ((y + 1) % ny) * 2 + (1 - z)), (z_far, ((y + 2) % ny) * 2 + (1 - z))]
    return done, late, side


def gradient(activations, cotangents, k, side=None, advance=None, z_light=False):
    tok_rows = activations[k, 0]
    cot_block = cotangents[k, 0]
    block = tok_rows.shape[0]
    d = lax.axis_index("dp")
    n_rows = tok_rows.shape[1] // 2
    dims = (((0,), (0,)), ((), ()))

    def partials(group):
        gathered = jnp.concatenate([blk for blk, _ in group])
        cot_rel = jnp.concatenate(
            [lax.dynamic_slice_in_dim(cot_block, src * block, block, axis=0) for _, src in group]
        )
        other = lax.dynamic_slice_in_dim(gathered, (1 - d) * n_rows, n_rows, axis=1)
        mine = lax.dynamic_slice_in_dim(gathered, d * n_rows, n_rows, axis=1)
        return (lax.dot_general(other, cot_rel, dims, preferred_element_type=jnp.float32),
                lax.dot_general(mine, cot_rel, dims, preferred_element_type=jnp.float32))

    (other_early, mine_early), late, side = gather_tokens(tok_rows, partials, side, advance, z_light)
    sent_early = lax.ppermute(other_early, "dp", [(0, 1), (1, 0)])
    other_late, mine_late = partials(late)
    sent_late = lax.ppermute(other_late, "dp", [(0, 1), (1, 0)])
    part_mine = lax.optimization_barrier(mine_early + mine_late + sent_early)
    return part_mine + sent_late, side


def x_hop(step):
    nx = 4

    def route_of(r):
        zh, x = divmod(r, nx)
        return zh * nx + (x + step) % nx
    return route_of


def trade_first(values):
    half = values.shape[0] // 2
    return (shifted(values[:half], "replica", x_hop(1)),
            shifted(values[half:], "replica", x_hop(-1)))


def trade_second(pair):
    a, b = pair
    return jnp.concatenate([shifted(a, "replica", x_hop(1)), shifted(b, "replica", x_hop(-1))])


def trade_with(level, values):
    if level == 1:
        return trade_second(trade_first(values))
    return swapped(values, "replica", level)


def stepped_of(grad, params_now, moment_now):
    moment_next = momentum_coef * moment_now + grad
    stepped = params_now - step_size * (grad + momentum_coef * moment_next)
    return stepped, moment_next


def trade_and_grad(level, stepped, activations, cotangents, k):
    if level == 1:
        grad, partner = gradient(activations, cotangents, k, trade_first(stepped), trade_second)
        return partner, grad
    return (swapped(stepped, "replica", level),
            gradient(activations, cotangents, k, z_light=level == 2)[0])


def local(round_index, activations, cotangents, params, momentum):
    params_now = params[0]
    moment_now = momentum[0]
    grad = gradient(activations, cotangents, 0)[0]
    for k in range(ROUNDS):
        stepped, moment_now = stepped_of(grad, params_now, moment_now)
        level = round_index[k] % 3
        if k + 1 < ROUNDS:
            branches = [partial(trade_and_grad, lv) for lv in range(3)]
            partner, grad = lax.switch(level, branches, stepped, activations, cotangents, k + 1)
        else:
            branches = [partial(trade_with, lv) for lv in range(3)]
            partner = lax.switch(level, branches, stepped)
        params_now = (stepped + partner) * 0.5
    return (params_now[None], moment_now[None])


def solution(mesh):
    in_specs = (
        P(),
        P(None, "replica", ("dp", "shard"), None),
        P(None, "replica", "dp", "shard"),
        P("replica", "dp", "shard"),
        P("replica", "dp", "shard"),
    )
    out_specs = (P("replica", "dp", "shard"), P("replica", "dp", "shard"))
    return jax.shard_map(local, mesh=mesh, in_specs=in_specs, out_specs=out_specs, check_vma=False)
```

```python
from functools import partial

import jax
import jax.numpy as jnp
from jax import lax
from jax.sharding import PartitionSpec as P

ROUNDS = 2


momentum_coef = 0.9
step_size = 0.25


def swapped(block, axis, stride):
    count = lax.axis_size(axis)
    route = []
    for low in range(count):
        high = low | 1 << stride
        if high != low and high < count:
            route += [(low, high), (high, low)]
    return lax.ppermute(block, axis, route)


def shifted(block, axis, route_of):
    count = lax.axis_size(axis)
    return lax.ppermute(block, axis, [(i, route_of(i)) for i in range(count)])


def gather_tokens(rows, first, side=None, advance=None, z_light=False):
    count = lax.axis_size("shard")
    ny = count // 2
    half = rows.shape[0] // 2

    def move(y_step, z_flip):
        def route_of(s):
            y, z = divmod(s, 2)
            return ((y + y_step) % ny) * 2 + (z ^ z_flip)
        return route_of

    z_in = shifted(rows, "shard", move(0, 1))
    from_dn = shifted(rows, "shard", move(1, 0))
    from_up = shifted(rows, "shard", move(-1, 0))
    if advance is not None:
        z_in, from_dn, from_up, side = lax.optimization_barrier((z_in, from_dn, from_up, side))
        side = advance(side)
    far_a = shifted(from_dn[:half], "shard", move(1, 0))
    far_b = shifted(from_up[half:], "shard", move(-1, 0))
    s = lax.axis_index("shard")
    y, z = s // 2, s % 2
    done = first([(rows, s), (z_in, y * 2 + (1 - z)), (from_dn, ((y - 1) % ny) * 2 + z),
                  (from_up, ((y + 1) % ny) * 2 + z)])
    far_a, far_b, z_in, done = lax.optimization_barrier((far_a, far_b, z_in, done))
    far = jnp.concatenate([far_a, far_b])
    if not z_light:
        z_far = shifted(far, "shard", move(0, 1))
    z_from_dn = shifted(z_in, "shard", move(1, 0))
    z_from_up = shifted(z_in, "shard", move(-1, 0))
    if z_light:
        z_far = jnp.concatenate([shifted(z_from_dn[:half], "shard", move(1, 0)),
                                 shifted(z_from_up[half:], "shard", move(-1, 0))])
    if side is not None:
        z_from_dn, z_from_up, side = lax.optimization_barrier((z_from_dn, z_from_up, side))
    late = [(far, ((y + 2) % ny) * 2 + z), (z_from_dn, ((y - 1) % ny) * 2 + (1 - z)),
            (z_from_up, ((y + 1) % ny) * 2 + (1 - z)), (z_far, ((y + 2) % ny) * 2 + (1 - z))]
    return done, late, side


def gradient(activations, cotangents, k, side=None, advance=None, z_light=False):
    tok_rows = activations[k, 0]
    cot_block = cotangents[k, 0]
    block = tok_rows.shape[0]
    d = lax.axis_index("dp")
    n_rows = tok_rows.shape[1] // 2
    dims = (((0,), (0,)), ((), ()))

    def partials(group):
        gathered = jnp.concatenate([blk for blk, _ in group])
        cot_rel = jnp.concatenate(
            [lax.dynamic_slice_in_dim(cot_block, src * block, block, axis=0) for _, src in group]
        )
        other = lax.dynamic_slice_in_dim(gathered, (1 - d) * n_rows, n_rows, axis=1)
        mine = lax.dynamic_slice_in_dim(gathered, d * n_rows, n_rows, axis=1)
        return (lax.dot_general(other, cot_rel, dims, preferred_element_type=jnp.float32),
                lax.dot_general(mine, cot_rel, dims, preferred_element_type=jnp.float32))

    (other_early, mine_early), late, side = gather_tokens(tok_rows, partials, side, advance, z_light)
    other_late, mine_late = partials(late)
    part_other = other_early + other_late
    sent = lax.ppermute(part_other, "dp", [(0, 1), (1, 0)])
    part_mine = lax.optimization_barrier(mine_early + mine_late)
    return part_mine + sent, side


def x_hop(step):
    nx = 4

    def route_of(r):
        zh, x = divmod(r, nx)
        return zh * nx + (x + step) % nx
    return route_of


def trade_first(values):
    half = values.shape[0] // 2
    return (shifted(values[:half], "replica", x_hop(1)),
            shifted(values[half:], "replica", x_hop(-1)))


def trade_second(pair):
    a, b = pair
    return jnp.concatenate([shifted(a, "replica", x_hop(1)), shifted(b, "replica", x_hop(-1))])


def trade_with(level, values):
    if level == 1:
        return trade_second(trade_first(values))
    return swapped(values, "replica", level)


def stepped_of(grad, params_now, moment_now):
    moment_next = momentum_coef * moment_now + grad
    stepped = params_now - step_size * (grad + momentum_coef * moment_next)
    return stepped, moment_next


def trade_and_grad(level, stepped, activations, cotangents, k):
    if level == 1:
        grad, partner = gradient(activations, cotangents, k, trade_first(stepped), trade_second)
        return partner, grad
    grad, partner = gradient(activations, cotangents, k, swapped(stepped, "replica", level),
                             z_light=level == 2)
    return partner, grad


def local(round_index, activations, cotangents, params, momentum):
    params_now = params[0]
    moment_now = momentum[0]
    grad = gradient(activations, cotangents, 0)[0]
    for k in range(ROUNDS):
        stepped, moment_now = stepped_of(grad, params_now, moment_now)
        level = round_index[k] % 3
        if k + 1 < ROUNDS:
            branches = [partial(trade_and_grad, lv) for lv in range(3)]
            partner, grad = lax.switch(level, branches, stepped, activations, cotangents, k + 1)
        else:
            branches = [partial(trade_with, lv) for lv in range(3)]
            partner = lax.switch(level, branches, stepped)
        params_now = (stepped + partner) * 0.5
    return (params_now[None], moment_now[None])


def solution(mesh):
    in_specs = (
        P(),
        P(None, "replica", ("dp", "shard"), None),
        P(None, "replica", "dp", "shard"),
        P("replica", "dp", "shard"),
        P("replica", "dp", "shard"),
    )
    out_specs = (P("replica", "dp", "shard"), P("replica", "dp", "shard"))
    return jax.shard_map(local, mesh=mesh, in_specs=in_specs, out_specs=out_specs, check_vma=False)
```

```python
from functools import partial

import jax
import jax.numpy as jnp
from jax import lax
from jax.sharding import PartitionSpec as P

ROUNDS = 2


momentum_coef = 0.9
step_size = 0.25


def swapped(block, axis, stride):
    count = lax.axis_size(axis)
    route = []
    for low in range(count):
        high = low | 1 << stride
        if high != low and high < count:
            route += [(low, high), (high, low)]
    return lax.ppermute(block, axis, route)


def shifted(block, axis, route_of):
    count = lax.axis_size(axis)
    return lax.ppermute(block, axis, [(i, route_of(i)) for i in range(count)])


def gather_tokens(rows, first, side=None, advance=None, z_light=False):
    count = lax.axis_size("shard")
    ny = count // 2
    half = rows.shape[0] // 2

    def move(y_step, z_flip):
        def route_of(s):
            y, z = divmod(s, 2)
            return ((y + y_step) % ny) * 2 + (z ^ z_flip)
        return route_of

    z_in = shifted(rows, "shard", move(0, 1))
    from_dn = shifted(rows, "shard", move(1, 0))
    from_up = shifted(rows, "shard", move(-1, 0))
    if advance is not None:
        z_in, from_dn, from_up, side = lax.optimization_barrier((z_in, from_dn, from_up, side))
        side = advance(side)
    far_a = shifted(from_dn[:half], "shard", move(1, 0))
    far_b = shifted(from_up[half:], "shard", move(-1, 0))
    s = lax.axis_index("shard")
    y, z = s // 2, s % 2
    done = first([(rows, s), (z_in, y * 2 + (1 - z)), (from_dn, ((y - 1) % ny) * 2 + z),
                  (from_up, ((y + 1) % ny) * 2 + z)])
    far_a, far_b, z_in, done = lax.optimization_barrier((far_a, far_b, z_in, done))
    far = jnp.concatenate([far_a, far_b])
    if not z_light:
        z_far = shifted(far, "shard", move(0, 1))
    z_from_dn = shifted(z_in, "shard", move(1, 0))
    z_from_up = shifted(z_in, "shard", move(-1, 0))
    if z_light:
        z_far = jnp.concatenate([shifted(z_from_dn[:half], "shard", move(1, 0)),
                                 shifted(z_from_up[half:], "shard", move(-1, 0))])
    if side is not None:
        z_from_dn, z_from_up, side = lax.optimization_barrier((z_from_dn, z_from_up, side))
    late = [(far, ((y + 2) % ny) * 2 + z), (z_from_dn, ((y - 1) % ny) * 2 + (1 - z)),
            (z_from_up, ((y + 1) % ny) * 2 + (1 - z)), (z_far, ((y + 2) % ny) * 2 + (1 - z))]
    return done, late, side


def gradient(activations, cotangents, k, side=None, advance=None, z_light=False):
    tok_rows = activations[k, 0]
    cot_block = cotangents[k, 0]
    block = tok_rows.shape[0]
    d = lax.axis_index("dp")
    n_rows = tok_rows.shape[1] // 2
    dims = (((0,), (0,)), ((), ()))

    def partials(group):
        gathered = jnp.concatenate([blk for blk, _ in group])
        cot_rel = jnp.concatenate(
            [lax.dynamic_slice_in_dim(cot_block, src * block, block, axis=0) for _, src in group]
        )
        other = lax.dynamic_slice_in_dim(gathered, (1 - d) * n_rows, n_rows, axis=1)
        mine = lax.dynamic_slice_in_dim(gathered, d * n_rows, n_rows, axis=1)
        return (lax.dot_general(other, cot_rel, dims, preferred_element_type=jnp.float32),
                lax.dot_general(mine, cot_rel, dims, preferred_element_type=jnp.float32))

    (other_early, mine_early), late, side = gather_tokens(tok_rows, partials, side, advance, z_light)
    other_late, mine_late = partials(late)
    part_other = other_early + other_late
    sent = lax.ppermute(part_other, "dp", [(0, 1), (1, 0)])
    part_mine = lax.optimization_barrier(mine_late)
    return mine_early + part_mine + sent, side


def x_hop(step):
    nx = 4

    def route_of(r):
        zh, x = divmod(r, nx)
        return zh * nx + (x + step) % nx
    return route_of


def trade_first(values):
    half = values.shape[0] // 2
    return (shifted(values[:half], "replica", x_hop(1)),
            shifted(values[half:], "replica", x_hop(-1)))


def trade_second(pair):
    a, b = pair
    return jnp.concatenate([shifted(a, "replica", x_hop(1)), shifted(b, "replica", x_hop(-1))])


def trade_with(level, values):
    if level == 1:
        return trade_second(trade_first(values))
    return swapped(values, "replica", level)


def stepped_of(grad, params_now, moment_now):
    moment_next = momentum_coef * moment_now + grad
    stepped = params_now - step_size * (grad + momentum_coef * moment_next)
    return stepped, moment_next


def trade_and_grad(level, stepped, activations, cotangents, k):
    if level == 1:
        grad, partner = gradient(activations, cotangents, k, trade_first(stepped), trade_second)
        return partner, grad
    grad, partner = gradient(activations, cotangents, k, swapped(stepped, "replica", level),
                             z_light=level == 2)
    return partner, grad


def local(round_index, activations, cotangents, params, momentum):
    params_now = params[0]
    moment_now = momentum[0]
    grad = gradient(activations, cotangents, 0)[0]
    for k in range(ROUNDS):
        stepped, moment_now = stepped_of(grad, params_now, moment_now)
        level = round_index[k] % 3
        if k + 1 < ROUNDS:
            branches = [partial(trade_and_grad, lv) for lv in range(3)]
            partner, grad = lax.switch(level, branches, stepped, activations, cotangents, k + 1)
        else:
            branches = [partial(trade_with, lv) for lv in range(3)]
            partner = lax.switch(level, branches, stepped)
        params_now = (stepped + partner) * 0.5
    return (params_now[None], moment_now[None])


def solution(mesh):
    in_specs = (
        P(),
        P(None, "replica", ("dp", "shard"), None),
        P(None, "replica", "dp", "shard"),
        P("replica", "dp", "shard"),
        P("replica", "dp", "shard"),
    )
    out_specs = (P("replica", "dp", "shard"), P("replica", "dp", "shard"))
    return jax.shard_map(local, mesh=mesh, in_specs=in_specs, out_specs=out_specs, check_vma=False)
```
